32 devices in a mesh: grp: 2 (over x), gx: 4 (over z), gy: 4 (over y, core).
Axes of the slice: x: 2, y: 2, z: 4, core: 2. Of those that a mesh axis runs over, the one named last changes fastest.
Arguments:
- theta_anomaly: float32 [192, 64, 128], P(('grp', 'gx'), 'gy'), may hold values from -4 to 4
- humidity_ratio: float32 [192, 64, 128], P(('grp', 'gx'), 'gy'), may hold values from 0.6 to 1.4
- zonal_velocity: float32 [192, 64, 128], P(('grp', 'gx'), 'gy'), may hold values from -1.8 to 1.8
- meridional_velocity: float32 [192, 64, 128], P(('grp', 'gx'), 'gy'), may hold values from -1.8 to 1.8
- vertical_velocity: float32 [192, 64, 128], P(('grp', 'gx'), 'gy'), may hold values from -1.8 to 1.8
- patch_processor_map: int32 [8, 4, 8], P(('grp', 'gx'), 'gy'), may hold values from 0 to 3, as said below
- particle_bucket_population: int32 [8, 4, 8], P(('grp', 'gx'), 'gy'), may hold values from 0 to 1024, as said below
- particle_size_quadratic: float32 [8, 4, 8, 1024], P(('grp', 'gx'), 'gy'), may hold values from 0.25 to 4
- represented_number: float32 [8, 4, 8, 1024], P(('grp', 'gx'), 'gy'), may hold values from 0.5 to 2
- particle_location_number: int32 [8, 4, 8, 1024], P(('grp', 'gx'), 'gy'), may hold values from 48 to 6095, as said below
Outputs:
- final_temperature: float32 [192, 64, 128], P(('grp', 'gx'), 'gy')
- final_vapour: float32 [192, 64, 128], P(('grp', 'gx'), 'gy')
- final_east: float32 [192, 64, 128], P(('grp', 'gx'), 'gy')
- final_north: float32 [192, 64, 128], P(('grp', 'gx'), 'gy')
- final_vertical: float32 [192, 64, 128], P(('grp', 'gx'), 'gy')
- final_size_quadratic: float32 [8, 4, 8, 1024], P(('grp', 'gx'), 'gy')
The draws below stay inside these ranges and needn't reach their ends.
Inputs may be any that keep to these rules, and one draw needn't show every extreme that they name: `patch_processor_map`: entry [a, y, b] is the index along gx of the device in the same row (same grp half, same gy) that holds the droplets of column block b of device (a, y). Different blocks of one device go to different owners, so one device sends at most 2 blocks to one owner; in every row some owner holds 2 blocks from every device of the row. `particle_bucket_population`: entry [a, y, r] counts the live droplets of slot r = s x 2 + t of the owner (a, y); they are the first ones of the slot. A slot that receives no block has none; every slot of an owner that holds 2 blocks from every device is full. `particle_location_number`: the cell within the slot's block, column 128 + level, with levels from 48 to 79. Within a slot the live droplets are sorted by column, and so are the others.
All inputs are finite; a program needn't handle non-finite values.
Results may differ from the reference program's by a relative error of at most 0.0003.
Values sent between devices are 32-bit elements; how exact they have to be, the bound alone decides.
A program may use at most 64 MiB of HBM per device.

```python
import math
import jax
import jax.numpy as jnp

CX = 24
VERTICAL_LAYERS = 128
NBD = 8
KLO = 48
KHI = 80
DPB = 1024
NSUB = 4
ITERS = 4
NSTEP = 1
XPEERS = 4
XTILES = 8
YTILES = 4
SPAN_COUNT_EAST = 192
SPAN_COUNT_NORTH = 64
BY = 2
BCOL = 48
SLOTS = 2
ROWSLOTS = 8


def wind_draw(key, salt):
    normals = jnp.clip(jax.random.normal(jax.random.fold_in(key, salt), (SPAN_COUNT_EAST, SPAN_COUNT_NORTH, VERTICAL_LAYERS), jnp.float32), -4.0, 4.0)
    x_place = jnp.arange(SPAN_COUNT_EAST, dtype=jnp.float32)
    y_place = jnp.arange(SPAN_COUNT_NORTH, dtype=jnp.float32)
    x_frac = x_place / max(SPAN_COUNT_EAST - 1, 1)
    y_frac = y_place / max(SPAN_COUNT_NORTH - 1, 1)
    amplitude = 0.05 * jnp.exp(jnp.log(3.0) * (x_frac[:, None] + y_frac[None, :]))
    return amplitude[..., None] * normals


def draw_zonal_velocity(key, part):
    return wind_draw(key, 21)


def draw_meridional_velocity(key, part):
    return wind_draw(key, 22)


def draw_vertical_velocity(key, part):
    return wind_draw(key, 23)


def plan_owners(key):
    groups = XTILES // XPEERS
    busiest = jax.random.randint(jax.random.fold_in(key, 11), (groups, 1, YTILES, 1), 0, XPEERS)
    spread = (NBD + SLOTS - 1) // SLOTS
    offsets = jax.random.randint(jax.random.fold_in(key, 12), (groups, XPEERS, YTILES, 1), 0, spread)
    blocks = jnp.arange(NBD, dtype=jnp.int32)
    owners = (busiest - offsets + blocks // SLOTS) % XPEERS
    return (owners, busiest)


def plan_counts(key):
    owners, busiest = plan_owners(key)
    target = jnp.arange(XPEERS, dtype=jnp.int32)
    slot_index = jnp.arange(SLOTS, dtype=jnp.int32)
    blocks = jnp.arange(NBD, dtype=jnp.int32)
    owner_rows = owners.transpose(0, 2, 1, 3)
    matches = (owner_rows[:, None, :, :, :, None] == target[None, :, None, None, None, None]) & ((blocks % SLOTS)[None, None, None, None, :, None] == slot_index[None, None, None, None, None, :])
    assigned = jnp.any(matches, axis=4)
    drawn_count = jax.random.randint(jax.random.fold_in(key, 13), assigned.shape, DPB // 4, DPB + 1)
    busy_owner = target[None, :, None, None, None] == busiest[..., None]
    counts = jnp.where(assigned, jnp.where(busy_owner, DPB, drawn_count), 0)
    return counts.reshape(XTILES, YTILES, ROWSLOTS)


def draw_patch_processor_map(key, part):
    owners, busiest = plan_owners(key)
    return owners.reshape(XTILES, YTILES, NBD).astype(jnp.int32)


def draw_particle_bucket_population(key, part):
    return plan_counts(key).astype(jnp.int32)


def draw_particle_location_number(key, part):
    counts = plan_counts(key)
    extent = (XTILES, YTILES, ROWSLOTS, DPB)
    column = jax.random.randint(jax.random.fold_in(key, 14), extent, 0, BCOL)
    alive_mask = jnp.arange(DPB, dtype=jnp.int32) < counts[..., None]
    ordered = jnp.sort(jnp.where(alive_mask, column, column + BCOL), axis=-1)
    column = jnp.where(ordered >= BCOL, ordered - BCOL, ordered)
    height = jax.random.randint(jax.random.fold_in(key, 15), extent, KLO, KHI)
    return (column * VERTICAL_LAYERS + height).astype(jnp.int32)


def level_of(key, shape, cuts, smallest, top_value):
    loudness = 1.0
    for dim, parts in cuts:
        draws = jax.random.uniform(jax.random.fold_in(jax.random.fold_in(key, 6), dim), (parts,), jnp.float32, smallest / len(cuts), top_value / len(cuts))
        loudness = loudness * jnp.repeat(jnp.exp(draws), shape[dim] // parts).reshape((-1,) + (1,) * (len(shape) - 1 - dim))
    return loudness


def gaussian(own_key, shape, scale, bound, split=(), kind=jnp.bfloat16):
    values = scale * jax.random.normal(own_key, shape, jnp.float32)
    if split:
        values = values * level_of(own_key, shape, split, -0.22, 0.18)
    return jnp.clip(values, -bound, bound).astype(kind)


def setup_inputs(seed: int = 0) -> dict:
    key_list = jax.random.split(jax.random.key(seed), 11)
    return {
        "theta_anomaly": gaussian(key_list[0], (SPAN_COUNT_EAST, SPAN_COUNT_NORTH, VERTICAL_LAYERS), 1.0, 4.0, ((0, 8), (1, 4)), jnp.float32),
        "humidity_ratio": jnp.clip(0.6 + 0.79999995 * jax.random.uniform(key_list[1], (SPAN_COUNT_EAST, SPAN_COUNT_NORTH, VERTICAL_LAYERS), jnp.float32) ** level_of(key_list[1], (SPAN_COUNT_EAST, SPAN_COUNT_NORTH, VERTICAL_LAYERS), ((0, 8), (1, 4)), -0.2, 0.2), 0.6, 1.4),
        "zonal_velocity": draw_zonal_velocity(jax.random.fold_in(key_list[10], 71), 0),
        "meridional_velocity": draw_meridional_velocity(jax.random.fold_in(key_list[10], 71), 0),
        "vertical_velocity": draw_vertical_velocity(jax.random.fold_in(key_list[10], 71), 0),
        "patch_processor_map": draw_patch_processor_map(jax.random.fold_in(key_list[10], 71), 0),
        "particle_bucket_population": draw_particle_bucket_population(jax.random.fold_in(key_list[10], 71), 0),
        "particle_size_quadratic": jnp.clip(jnp.exp(math.log(4.0) - 2.7725887 * jax.random.uniform(key_list[7], (XTILES, YTILES, ROWSLOTS, DPB), jnp.float32) ** level_of(key_list[7], (XTILES, YTILES, ROWSLOTS, DPB), ((0, 8), (1, 4)), -0.2, 0.2)), 0.25, 4.0),
        "represented_number": jnp.clip(jnp.exp(math.log(2.0) - 1.3862944 * jax.random.uniform(key_list[8], (XTILES, YTILES, ROWSLOTS, DPB), jnp.float32) ** level_of(key_list[8], (XTILES, YTILES, ROWSLOTS, DPB), ((0, 8), (1, 4)), -0.2, 0.2)), 0.5, 2.0),
        "particle_location_number": draw_particle_location_number(jax.random.fold_in(key_list[10], 71), 0),
    }


TIME_INCREMENT = 0.15
THERMAL_LIFT = 0.5
HUMID_LIFT = 0.3
HELMHOLTZ = 0.001
CLAUSIUS_FACTOR = 0.2
GROWTH = 0.5
GROWTH_SLOPE = 0.1
SUB_STEP = 0.25
CURVATURE = 0.05
FLOOR_SQUARE = 0.04
CONDENSE = 0.2
PHASE_WARMING = 2.5

def profiles():
    heights = jnp.arange(VERTICAL_LAYERS, dtype=jnp.float32)
    midpoint_mass_per_volume = jnp.exp(-(heights + 0.5) / VERTICAL_LAYERS)
    interface_mass_per_volume = jnp.where(heights < VERTICAL_LAYERS - 1, jnp.exp(-(heights + 1.0) / VERTICAL_LAYERS), 0.0)
    return (midpoint_mass_per_volume, interface_mass_per_volume)

def level_above(values):
    return jnp.concatenate([values[..., 1:], jnp.zeros_like(values[..., :1])], axis=-1)

def level_below(values):
    return jnp.concatenate([jnp.zeros_like(values[..., :1]), values[..., :-1]], axis=-1)

def beside_all(values):
    return (jnp.roll(values, -1, 0), jnp.roll(values, 1, 0), jnp.roll(values, -1, 1), jnp.roll(values, 1, 1))

def operate(values, midpoint_mass_per_volume, interface_mass_per_volume):
    east_side, west_side, north_side, south_side = beside_all(values)
    return midpoint_mass_per_volume * ((4.0 + HELMHOLTZ) * values - east_side - west_side - north_side - south_side) + interface_mass_per_volume * (values - level_above(values)) + level_below(interface_mass_per_volume) * (values - level_below(values))

def solve_pressure(right_side, midpoint_mass_per_volume, interface_mass_per_volume):
    potential = jnp.zeros_like(right_side)
    residual = right_side
    direction = right_side
    norm_now = jnp.sum(residual * residual)
    for iteration in range(ITERS):
        applied = operate(direction, midpoint_mass_per_volume, interface_mass_per_volume)
        step_length = norm_now / jnp.sum(direction * applied)
        potential = potential + step_length * direction
        residual = residual - step_length * applied
        norm_next = jnp.sum(residual * residual)
        direction = residual + norm_next / norm_now * direction
        norm_now = norm_next
    return potential

def advect_scalars(values, zonal_velocity, meridional_velocity, vertical_velocity):
    east_side, west_side, north_side, south_side = beside_all(values)
    lower_level = jnp.concatenate([values[..., :1], values[..., :-1]], axis=-1)
    upper_level = jnp.concatenate([values[..., 1:], values[..., -1:]], axis=-1)
    tendency = jnp.maximum(zonal_velocity, 0.0) * (values - west_side) + jnp.minimum(zonal_velocity, 0.0) * (east_side - values) + jnp.maximum(meridional_velocity, 0.0) * (values - south_side) + jnp.minimum(meridional_velocity, 0.0) * (north_side - values) + jnp.maximum(vertical_velocity, 0.0) * (values - lower_level) + jnp.minimum(vertical_velocity, 0.0) * (upper_level - values)
    return values - TIME_INCREMENT * tendency

def grow_droplets(supersat_ratio, warmth, particle_size_quadratic, represented_number, alive_mask):
    growth_rate = GROWTH * jnp.exp(GROWTH_SLOPE * warmth)
    square_now = particle_size_quadratic
    for substep in range(NSUB):
        square_now = jnp.maximum(square_now + 2.0 * SUB_STEP * growth_rate * (supersat_ratio - CURVATURE / jnp.sqrt(square_now)), FLOOR_SQUARE)
    grown_square = jnp.where(alive_mask, square_now, particle_size_quadratic)
    mass_change = jnp.where(alive_mask, represented_number * (grown_square * jnp.sqrt(grown_square) - particle_size_quadratic * jnp.sqrt(particle_size_quadratic)), 0.0)
    return (grown_square, mass_change)

def into_patches(values):
    shaped = values.reshape(XTILES, CX, YTILES, NBD, BY, VERTICAL_LAYERS)
    return shaped.transpose(0, 2, 3, 1, 4, 5).reshape(XTILES, YTILES, NBD, BCOL * VERTICAL_LAYERS)

def from_blocks(blocks):
    shaped = blocks.reshape(XTILES, YTILES, NBD, CX, BY, VERTICAL_LAYERS)
    return shaped.transpose(0, 3, 1, 2, 4, 5).reshape(SPAN_COUNT_EAST, SPAN_COUNT_NORTH, VERTICAL_LAYERS)

def reference(theta_anomaly, humidity_ratio, zonal_velocity, meridional_velocity, vertical_velocity, patch_processor_map, particle_bucket_population, particle_size_quadratic, represented_number, particle_location_number):
    midpoint_mass_per_volume, interface_mass_per_volume = profiles()
    tile_x = jnp.arange(XTILES, dtype=jnp.int32)[:, None, None]
    tile_y = jnp.arange(YTILES, dtype=jnp.int32)[None, :, None]
    block_index = jnp.arange(NBD, dtype=jnp.int32)[None, None, :]
    owner_row = (tile_x // XPEERS * XPEERS + patch_processor_map).astype(jnp.int32)
    slot_index = (tile_x % XPEERS * SLOTS + block_index % SLOTS).astype(jnp.int32)
    row_y = jnp.broadcast_to(tile_y, patch_processor_map.shape).astype(jnp.int32)
    block_count = particle_bucket_population[owner_row, row_y, slot_index]
    patch_location = particle_location_number[owner_row, row_y, slot_index]
    block_mult = represented_number[owner_row, row_y, slot_index]
    block_radius = particle_size_quadratic[owner_row, row_y, slot_index]
    alive_mask = jnp.arange(DPB, dtype=jnp.int32) < block_count[..., None]
    offsets = (jnp.arange(XTILES * YTILES * NBD, dtype=jnp.int32) * (BCOL * VERTICAL_LAYERS)).reshape(XTILES, YTILES, NBD, 1)
    flat_cell = (patch_location + offsets).reshape(-1)
    for stepping in range(NSTEP):
        raised_airmass = vertical_velocity + TIME_INCREMENT * (THERMAL_LIFT * theta_anomaly + HUMID_LIFT * humidity_ratio)
        divergence = midpoint_mass_per_volume * ((jnp.roll(zonal_velocity, -1, 0) - jnp.roll(zonal_velocity, 1, 0)) * 0.5 + (jnp.roll(meridional_velocity, -1, 1) - jnp.roll(meridional_velocity, 1, 1)) * 0.5) + 0.5 * (level_above(midpoint_mass_per_volume * raised_airmass) - level_below(midpoint_mass_per_volume * raised_airmass))
        potential = solve_pressure(-divergence / TIME_INCREMENT, midpoint_mass_per_volume, interface_mass_per_volume)
        zonal_velocity = zonal_velocity - TIME_INCREMENT * 0.5 * (jnp.roll(potential, -1, 0) - jnp.roll(potential, 1, 0))
        meridional_velocity = meridional_velocity - TIME_INCREMENT * 0.5 * (jnp.roll(potential, -1, 1) - jnp.roll(potential, 1, 1))
        vertical_velocity = raised_airmass - TIME_INCREMENT * 0.5 * (level_above(potential) - level_below(potential))
        advected_theta = advect_scalars(theta_anomaly, zonal_velocity, meridional_velocity, vertical_velocity)
        advected_humidity = advect_scalars(humidity_ratio, zonal_velocity, meridional_velocity, vertical_velocity)
        supersat_ratio = advected_humidity * jnp.exp(-CLAUSIUS_FACTOR * advected_theta) - 1.0
        sat_drops = jnp.take_along_axis(into_patches(supersat_ratio), patch_location, axis=3)
        grow_particles = jnp.take_along_axis(into_patches(advected_theta), patch_location, axis=3)
        block_radius, mass_change = grow_droplets(sat_drops, grow_particles, block_radius, block_mult, alive_mask)
        liquid_content = CONDENSE * jax.ops.segment_sum(mass_change.reshape(-1), flat_cell, num_segments=XTILES * YTILES * NBD * BCOL * VERTICAL_LAYERS)
        liquid_content = from_blocks(liquid_content.reshape(XTILES, YTILES, NBD, BCOL * VERTICAL_LAYERS))
        theta_anomaly = advected_theta + PHASE_WARMING * liquid_content
        humidity_ratio = advected_humidity - liquid_content
    final_size_quadratic = particle_size_quadratic.at[owner_row, row_y, slot_index].set(block_radius)
    return (theta_anomaly, humidity_ratio, zonal_velocity, meridional_velocity, vertical_velocity, final_size_quadratic)
```

```python
import functools

import jax
import jax.numpy as jnp
from jax import lax
from jax.experimental import pallas as pl
from jax.experimental.pallas import tpu as pltpu
from jax.sharding import PartitionSpec as P

NBD = 8
NSUB = 4
ITERS = 4
KLO = 48
KHI = 80

DT = 0.15
THERMAL_LIFT = 0.5
HUMID_LIFT = 0.3
HELMHOLTZ = 0.001
CLAUSIUS_FACTOR = 0.2
GROWTH = 0.5
GROWTH_SLOPE = 0.1
SUB_STEP = 0.25
CURVATURE = 0.05
FLOOR_SQUARE = 0.04
CONDENSE = 0.2
PHASE_WARMING = 2.5

H = 5
HY = 8
MESH = pl.DeviceIdType.MESH
HIGH = lax.Precision.HIGHEST


def cg_coefficients(m):
    def inner(a, b):
        total = None
        for i, ai in enumerate(a):
            part = None
            for j, bj in enumerate(b):
                term = bj * (0.5 * (m[i + j] + m[abs(i - j)]))
                part = term if part is None else part + term
            part = ai * part
            total = part if total is None else total + part
        return total

    one = jnp.ones_like(m[0])
    zero = jnp.zeros_like(m[0])

    def apply(d):
        out = [zero] * (len(d) + 1)
        for i, di in enumerate(d):
            out[i] = out[i] + 6.0 * di
            if i == 0:
                out[1] = out[1] + 6.0 * di
            else:
                out[i + 1] = out[i + 1] + 3.0 * di
                out[i - 1] = out[i - 1] + 3.0 * di
        return out

    res, d, pot, rr = [one], [one], [], m[0]
    for it in range(ITERS):
        img = apply(d)
        alpha = rr / inner(d, img)
        pot = [
            alpha * d[i] + (pot[i] if i < len(pot) else 0.0) for i in range(len(d))
        ]
        if it + 1 == ITERS:
            break
        res = [(res[i] if i < len(res) else zero) - alpha * img[i] for i in range(len(img))]
        new = inner(res, res)
        beta = new / rr
        d = [res[i] + (beta * d[i] if i < len(d) else 0.0) for i in range(len(res))]
        rr = new
    return pot


def kernel(
    ngrp, ngx, ngy, slots,
    t_ref, q_ref, u_ref, v_ref, w_ref, map_ref, cnt_ref, size_ref, mult_ref, cell_ref,
    to_ref, qo_ref, uo_ref, vo_ref, wo_ref, so_ref,
    ue, ve, le, te, qe, p0, p1, p2, p3, pack, got, part, got_x, part2, got_y,
    blk, out1, in1, sat_s, tmp_s, out2, in2, cond, grid_c, packed,
    send_sem, recv_sem,
):
    cx, cy, nz = t_ref.shape
    rows = 2 * HY + cy
    grp, gx, gy = lax.axis_index("grp"), lax.axis_index("gx"), lax.axis_index("gy")
    nx = ngrp * ngx
    xt = grp * ngx + gx

    def dev(dx, dy):
        other = lax.rem(xt + dx + nx, nx)
        return (lax.div(other, ngx), lax.rem(other, ngx), lax.rem(gy + dy + ngy, ngy))

    barrier = pltpu.get_barrier_semaphore()
    greet = [dev(o, 0) for o in range(1, nx)] + [dev(0, o) for o in range(1, ngy)]
    greet += [dev(a, b) for a in (-1, 1) for b in (-1, 1)]
    greet += []
    for target in greet:
        pl.semaphore_signal(barrier, inc=1, device_id=target, device_id_type=MESH)

    own = slice(HY, HY + cy)

    def stage(x, c):
        tt, qq, uu, vv = t_ref[x], q_ref[x], u_ref[x], v_ref[x]
        lift = w_ref[x] + DT * (THERMAL_LIFT * tt + HUMID_LIFT * qq)
        ue[x + H, own, :] = uu
        ve[x + H, own, :] = vv
        le[x + H, own, :] = lift
        te[x + H, own, :] = tt
        qe[x + H, own, :] = qq
        pack[0, x, 0:4, :] = uu[cy - 4 :]
        pack[0, x, 4:9, :] = vv[cy - 5 :]
        pack[0, x, 9:13, :] = lift[cy - 4 :]
        pack[0, x, 13:14, :] = tt[cy - 1 :]
        pack[0, x, 14:15, :] = qq[cy - 1 :]
        pack[1, x, 0:4, :] = uu[0:4]
        pack[1, x, 4:9, :] = vv[0:5]
        pack[1, x, 9:13, :] = lift[0:4]
        pack[1, x, 13:14, :] = tt[0:1]
        pack[1, x, 14:15, :] = qq[0:1]
        return c

    lax.fori_loop(0, cx, stage, 0)
    pl.semaphore_wait(barrier, len(greet))

    sems = [0]
    started = []

    def send(src, dst, target):
        i = sems[0]
        sems[0] += 1
        copy = pltpu.make_async_remote_copy(
            src_ref=src, dst_ref=dst, send_sem=send_sem.at[i], recv_sem=recv_sem.at[i],
            device_id=target, device_id_type=MESH,
        )
        copy.start()
        started.append(copy)
        return copy

    e = H + cx
    halo = []
    east, west = dev(1, 0), dev(-1, 0)
    halo.append(send(u_ref.at[pl.ds(cx - 5, 5)], ue.at[pl.ds(0, 5), own], east))
    halo.append(send(u_ref.at[pl.ds(0, 5)], ue.at[pl.ds(e, 5), own], west))
    halo.append(send(v_ref.at[pl.ds(cx - 4, 4)], ve.at[pl.ds(1, 4), own], east))
    halo.append(send(v_ref.at[pl.ds(0, 4)], ve.at[pl.ds(e, 4), own], west))
    halo.append(send(le.at[pl.ds(e - 4, 4), own], le.at[pl.ds(1, 4), own], east))
    halo.append(send(le.at[pl.ds(H, 4), own], le.at[pl.ds(e, 4), own], west))
    halo.append(send(pack.at[0], got.at[0, pl.ds(H, cx)], dev(0, 1)))
    halo.append(send(pack.at[1], got.at[1, pl.ds(H, cx)], dev(0, -1)))
    for a, dy in ((0, 1), (1, -1)):
        halo.append(send(pack.at[a, pl.ds(cx - 5, 5)], got.at[a, pl.ds(0, 5)], dev(1, dy)))
        halo.append(send(pack.at[a, pl.ds(0, 5)], got.at[a, pl.ds(e, 5)], dev(-1, dy)))
    for src, dst in ((t_ref, te), (q_ref, qe)):
        halo.append(send(src.at[pl.ds(cx - 1, 1)], dst.at[pl.ds(H - 1, 1), own], east))
        halo.append(send(src.at[pl.ds(0, 1)], dst.at[pl.ds(e, 1), own], west))

    lane = lax.broadcasted_iota(jnp.int32, (1, nz), 1)
    height = lane.astype(jnp.float32)
    rho = jnp.exp(-(height + 0.5) / nz)
    face = jnp.where(lane < nz - 1, jnp.exp(-(height + 1.0) / nz), 0.0)
    face_dn = jnp.where(lane > 0, jnp.exp(-height / nz), 0.0)
    not_top = jnp.where(lane < nz - 1, 1.0, 0.0)
    not_bot = jnp.where(lane > 0, 1.0, 0.0)
    rho_up = jnp.where(lane < nz - 1, jnp.exp(-(height + 1.5) / nz), 0.0)
    rho_dn = jnp.where(lane > 0, jnp.exp(-(height - 0.5) / nz), 0.0)

    def up(f):
        return pltpu.roll(f, nz - 1, 1)

    def down(f):
        return pltpu.roll(f, 1, 1)

    for copy in halo:
        copy.wait_recv()

    def unpack(x, c):
        s, n = got[0, x], got[1, x]
        ue[x, HY - 4 : HY, :] = s[0:4]
        ve[x, HY - 5 : HY, :] = s[4:9]
        le[x, HY - 4 : HY, :] = s[9:13]
        te[x, HY - 1 : HY, :] = s[13:14]
        qe[x, HY - 1 : HY, :] = s[14:15]
        ue[x, HY + cy : HY + cy + 4, :] = n[0:4]
        ve[x, HY + cy : HY + cy + 5, :] = n[4:9]
        le[x, HY + cy : HY + cy + 4, :] = n[9:13]
        te[x, HY + cy : HY + cy + 1, :] = n[13:14]
        qe[x, HY + cy : HY + cy + 1, :] = n[14:15]
        return c

    lax.fori_loop(0, cx + 2 * H, unpack, 0)

    def make_r(x, c):
        vv, ll = ve[x], le[x]
        horiz = (ue[x + 1] - ue[x - 1]) + (pltpu.roll(vv, rows - 1, 0) - pltpu.roll(vv, 1, 0))
        div = rho * (0.5 * horiz) + 0.5 * (rho_up * up(ll) - rho_dn * down(ll))
        p0[x] = div * (-1.0 / DT)
        return c

    lax.fori_loop(1, cx + 2 * H - 1, make_r, 0)

    diag = ((4.0 + HELMHOLTZ) * rho + face + face_dn) / 6.0 - 1.0
    rho6, face6, face_dn6 = rho / 6.0, face / 6.0, face_dn / 6.0

    def scaled(f, x):
        c = f[x]
        side = f[x + 1] + f[x - 1] + pltpu.roll(c, rows - 1, 0) + pltpu.roll(c, 1, 0)
        return diag * c - rho6 * side - face6 * up(c) - face_dn6 * down(c)

    def step1(x, c):
        p1[x] = scaled(p0, x)
        return c

    def step2(x, c):
        p2[x] = 2.0 * scaled(p1, x) - p0[x]
        return c

    def step3(x, c):
        p3[x] = 2.0 * scaled(p2, x) - p1[x]
        return c

    full = cx + 2 * H
    lax.fori_loop(2, full - 2, step1, 0)
    lax.fori_loop(3, full - 3, step2, 0)
    lax.fori_loop(4, full - 4, step3, 0)

    def dots(x, acc):
        a0, a1, a2, a3 = p0[x, own, :], p1[x, own, :], p2[x, own, :], p3[x, own, :]
        side = p3[x + 1, own, :] + p3[x - 1, own, :]
        side = side + p3[x, HY - 1 : HY + cy - 1, :] + p3[x, HY + 1 : HY + cy + 1, :]
        a4 = 2.0 * (diag * a3 - rho6 * side - face6 * up(a3) - face_dn6 * down(a3)) - a2
        pairs = ((a0, a0), (a0, a1), (a1, a1), (a1, a2), (a2, a2), (a2, a3), (a3, a3), (a3, a4))
        return tuple(s + f * g for s, (f, g) in zip(acc, pairs))

    acc = lax.fori_loop(H, e, dots, (jnp.zeros((cy, nz), jnp.float32),) * 8)
    for i in range(8):
        part[i : i + 1, :] = jnp.sum(acc[i], axis=0, keepdims=True)

    peers = [send(part, got_x.at[o - 1], dev(o, 0)) for o in range(1, nx)]
    total = part[...]
    for o, copy in enumerate(peers):
        copy.wait_recv()
        total = total + got_x[o]
    part2[...] = total
    peers = [send(part2, got_y.at[o - 1], dev(0, o)) for o in range(1, ngy)]
    for o, copy in enumerate(peers):
        copy.wait_recv()
        total = total + got_y[o]
    total = jnp.broadcast_to(jnp.sum(total, axis=1, keepdims=True), (8, nz))
    dot = [total[i : i + 1, :] for i in range(8)]
    m = [dot[0], dot[1]]
    for k in range(2, 8):
        m.append(2.0 * dot[k] - m[k % 2])
    c0, c1, c2, c3 = cg_coefficients(m)

    def potential(x, c):
        p0[x] = c0 * p0[x] + c1 * p1[x] + c2 * p2[x] + c3 * p3[x]
        return c

    lax.fori_loop(H - 1, e + 1, potential, 0)

    sub = lax.broadcasted_iota(jnp.int32, (cy, nz), 0)
    lanes = lax.broadcasted_iota(jnp.int32, (cy, nz), 1)
    nlev = KHI - KLO
    half = 2 * nlev
    south = slice(HY - 1, HY + cy - 1)
    north = slice(HY + 1, HY + cy + 1)

    def advance(x, c):
        g = x + H
        phi = p0[g, own, :]
        u = ue[g, own, :] - (DT * 0.5) * (p0[g + 1, own, :] - p0[g - 1, own, :])
        v = ve[g, own, :] - (DT * 0.5) * (p0[g, north, :] - p0[g, south, :])
        w = le[g, own, :] - (DT * 0.5) * (not_top * up(phi) - not_bot * down(phi))
        uo_ref[x] = u
        vo_ref[x] = v
        wo_ref[x] = w
        u_p, u_m = jnp.maximum(u, 0.0), jnp.minimum(u, 0.0)
        v_p, v_m = jnp.maximum(v, 0.0), jnp.minimum(v, 0.0)
        w_p, w_m = jnp.maximum(w, 0.0) * not_bot, jnp.minimum(w, 0.0) * not_top

        def move(f):
            h = f[g, own, :]
            return h - DT * (
                u_p * (h - f[g - 1, own, :])
                + u_m * (f[g + 1, own, :] - h)
                + v_p * (h - f[g, south, :])
                + v_m * (f[g, north, :] - h)
                + w_p * (h - down(h))
                + w_m * (up(h) - h)
            )

        tt, qq = move(te), move(qe)
        to_ref[x] = tt
        qo_ref[x] = qq
        sat = qq * jnp.exp(-CLAUSIUS_FACTOR * tt) - 1.0
        both = jnp.where(
            lanes < nlev, pltpu.roll(sat, nz - KLO, 1), pltpu.roll(tt, nz - KLO + nlev, 1)
        )
        odd = pltpu.roll(pltpu.roll(both, cy - 1, 0), half, 1)
        packed[x] = jnp.where(lanes < half, both, odd)
        return c

    lax.fori_loop(0, cx, advance, 0)
    for x in range(cx):
        for b in range(NBD):
            blk[b, x : x + 1, :] = packed[x, 2 * b : 2 * b + 1, :]

    nrow = ngx * slots
    for r in range(nrow):
        o, t = r // slots, r % slots
        row = None
        for b in range(t, NBD, slots):
            term = jnp.where(map_ref[0, b] == o, 1.0, 0.0) * blk[b]
            row = term if row is None else row + term
        out1[r] = row

    def exchange(src, dst):
        copies = []
        for o in range(1, ngx):
            other = lax.rem(gx + o, ngx)
            copies.append(
                send(
                    src.at[pl.ds(other * slots, slots)],
                    dst.at[pl.ds(gx * slots, slots)],
                    (grp, other, gy),
                )
            )
        for t in range(slots):
            dst[gx * slots + t] = src[gx * slots + t]
        for copy in copies:
            copy.wait_recv()

    exchange(out1, in1)

    dpb = size_ref.shape[1]
    wide = lax.broadcasted_iota(jnp.int32, (nz, dpb), 0)
    narrow = lax.broadcasted_iota(jnp.int32, (cx, dpb), 0)

    def place(r):
        cell = cell_ref[pl.ds(r, 1), :]
        lx = cell // (2 * nz)
        s = (cell // nz) % 2 * half + cell % nz - KLO
        return jnp.where(narrow == lx, 1.0, 0.0), s

    for r in range(nrow):
        hot, s = place(r)
        res = lax.dot_general(
            in1[r], hot, (((0,), (0,)), ((), ())), precision=HIGH,
            preferred_element_type=jnp.float32,
        )
        sat_s[r : r + 1, :] = jnp.sum(jnp.where(wide == s, res, 0.0), axis=0, keepdims=True)
        tmp_s[r : r + 1, :] = jnp.sum(
            jnp.where(wide == s + nlev, res, 0.0), axis=0, keepdims=True
        )

    rate = (2.0 * SUB_STEP * GROWTH) * jnp.exp(GROWTH_SLOPE * tmp_s[...])
    gain = rate * sat_s[...]
    loss = rate * CURVATURE
    old = size_ref[...]
    x2 = old
    for _ in range(NSUB):
        x2 = jnp.maximum(x2 + gain - loss * lax.rsqrt(x2), FLOOR_SQUARE)
    alive = lax.broadcasted_iota(jnp.int32, (nrow, dpb), 1) < cnt_ref[...]
    new = jnp.where(alive, x2, old)
    so_ref[...] = new
    sat_s[...] = jnp.where(
        alive,
        CONDENSE * mult_ref[...] * (new * jnp.sqrt(new) - old * jnp.sqrt(old)),
        0.0,
    )

    for r in range(nrow):
        hot, s = place(r)
        mass = jnp.where(wide == s, sat_s[r : r + 1, :], 0.0)
        out2[r] = lax.dot_general(
            hot, mass, (((1,), (1,)), ((), ())), precision=HIGH,
            preferred_element_type=jnp.float32,
        )

    exchange(out2, in2)

    for b in range(NBD):
        acc = None
        for o in range(ngx):
            term = jnp.where(map_ref[0, b] == o, 1.0, 0.0) * in2[o * slots + b % slots]
            acc = term if acc is None else acc + term
        cond[b] = acc
    for x in range(cx):
        for b in range(NBD):
            line = cond[b, x : x + 1, :]
            grid_c[x, 2 * b : 2 * b + 1, :] = line
            grid_c[x, 2 * b + 1 : 2 * b + 2, :] = line

    even = sub % 2 == 0
    inside = (lanes >= KLO) & (lanes < KHI)

    def finish(x, c):
        f = grid_c[x]
        f = jnp.where(even, pltpu.roll(f, KLO, 1), pltpu.roll(f, nz + KLO - half, 1))
        f = jnp.where(inside, f, 0.0)
        to_ref[x] = to_ref[x] + PHASE_WARMING * f
        qo_ref[x] = qo_ref[x] - f
        return c

    lax.fori_loop(0, cx, finish, 0)
    for copy in started:
        copy.wait_send()


def on_device(ngrp, ngx, ngy, t, q, u, v, w, owner, count, size, mult, cell):
    cx, cy, nz = t.shape
    nrow, dpb = size.shape[2:]
    slots = nrow // ngx
    ext = pltpu.VMEM((cx + 2 * H, cy + 2 * HY, nz), jnp.float32)
    rowbuf = pltpu.VMEM((nrow, cx, nz), jnp.float32)
    vec = pltpu.VMEM((nrow, dpb), jnp.float32)
    nsem = 16 + (ngrp * ngx - 1) + (ngy - 1) + 2 * (ngx - 1)
    grid = jax.ShapeDtypeStruct((cx, cy, nz), jnp.float32)
    vm = pl.BlockSpec(memory_space=pltpu.VMEM)
    sm = pl.BlockSpec(memory_space=pltpu.SMEM)
    outs = pl.pallas_call(
        functools.partial(kernel, ngrp, ngx, ngy, slots),
        out_shape=(grid,) * 5 + (jax.ShapeDtypeStruct((nrow, dpb), jnp.float32),),
        in_specs=[vm] * 5 + [sm] + [vm] * 4,
        out_specs=(vm,) * 6,
        scratch_shapes=[
            ext, ext, ext, ext, ext, ext, ext, ext, ext,
            pltpu.VMEM((2, cx, 16, nz), jnp.float32),
            pltpu.VMEM((2, cx + 2 * H, 16, nz), jnp.float32),
            pltpu.VMEM((8, nz), jnp.float32),
            pltpu.VMEM((ngrp * ngx - 1, 8, nz), jnp.float32),
            pltpu.VMEM((8, nz), jnp.float32),
            pltpu.VMEM((ngy - 1, 8, nz), jnp.float32),
            pltpu.VMEM((NBD, cx, nz), jnp.float32),
            rowbuf, rowbuf, vec, vec, rowbuf, rowbuf,
            pltpu.VMEM((NBD, cx, nz), jnp.float32),
            pltpu.VMEM((cx, cy, nz), jnp.float32),
            pltpu.VMEM((cx, cy, nz), jnp.float32),
            pltpu.SemaphoreType.DMA((nsem,)),
            pltpu.SemaphoreType.DMA((nsem,)),
        ],
        compiler_params=pltpu.CompilerParams(collective_id=0, has_side_effects=True),
        name="cloud_step",
    )(
        t, q, u, v, w, owner.reshape(1, -1), count.reshape(nrow, 1),
        size[0, 0], mult[0, 0], cell[0, 0],
    )
    return outs[:5] + (outs[5][None, None],)


def solution(mesh):
    grid = P(("grp", "gx"), "gy", None)
    drop = P(("grp", "gx"), "gy", None, None)
    return jax.shard_map(
        functools.partial(on_device, mesh.shape["grp"], mesh.shape["gx"], mesh.shape["gy"]),
        mesh=mesh,
        in_specs=(grid,) * 7 + (drop,) * 3,
        out_specs=(grid,) * 5 + (drop,),
        check_vma=False,
    )
```

```python
import functools

import jax
import jax.numpy as jnp
from jax import lax
from jax.experimental import pallas as pl
from jax.experimental.pallas import tpu as pltpu
from jax.sharding import PartitionSpec as P

NBD = 8
NSUB = 4
ITERS = 4
KLO = 48
KHI = 80

DT = 0.15
THERMAL_LIFT = 0.5
HUMID_LIFT = 0.3
HELMHOLTZ = 0.001
CLAUSIUS_FACTOR = 0.2
GROWTH = 0.5
GROWTH_SLOPE = 0.1
SUB_STEP = 0.25
CURVATURE = 0.05
FLOOR_SQUARE = 0.04
CONDENSE = 0.2
PHASE_WARMING = 2.5

H = 5
HY = 8
MESH = pl.DeviceIdType.MESH


def sweep(lo, hi, body, k=8):
    turns = (hi - lo) // k

    def turn(i, c):
        for j in range(k):
            body(lo + i * k + j)
        return c

    lax.fori_loop(0, turns, turn, 0)
    for x in range(lo + turns * k, hi):
        body(x)


def cg_coefficients(m):
    def inner(a, b):
        total = None
        for i, ai in enumerate(a):
            part = None
            for j, bj in enumerate(b):
                term = bj * (0.5 * (m[i + j] + m[abs(i - j)]))
                part = term if part is None else part + term
            part = ai * part
            total = part if total is None else total + part
        return total

    one = jnp.ones_like(m[0])
    zero = jnp.zeros_like(m[0])

    def apply(d):
        out = [zero] * (len(d) + 1)
        for i, di in enumerate(d):
            out[i] = out[i] + 6.0 * di
            if i == 0:
                out[1] = out[1] + 6.0 * di
            else:
                out[i + 1] = out[i + 1] + 3.0 * di
                out[i - 1] = out[i - 1] + 3.0 * di
        return out

    res, d, pot, rr = [one], [one], [], m[0]
    for it in range(ITERS):
        img = apply(d)
        alpha = rr / inner(d, img)
        pot = [
            alpha * d[i] + (pot[i] if i < len(pot) else 0.0) for i in range(len(d))
        ]
        if it + 1 == ITERS:
            break
        res = [(res[i] if i < len(res) else zero) - alpha * img[i] for i in range(len(img))]
        new = inner(res, res)
        beta = new / rr
        d = [res[i] + (beta * d[i] if i < len(d) else 0.0) for i in range(len(res))]
        rr = new
    return pot


def kernel(
    ngrp, ngx, ngy, slots,
    t_ref, q_ref, u_ref, v_ref, w_ref, map_ref, cnt_ref, size_ref, mult_ref, cell_ref,
    to_ref, qo_ref, uo_ref, vo_ref, wo_ref, so_ref, cond,
    ue, ve, le, te, qe, p0, p1, p2, p3, phi_s, pack, got, part, got_x,
    blk, out1, in1, sat_s, tmp_s, live_s, lev_s, hot_s, out2, in2, packed,
    send_sem, recv_sem, sum_send, sum_recv,
):
    cx, cy, nz = t_ref.shape
    rows = 2 * HY + cy
    grp, gx, gy = lax.axis_index("grp"), lax.axis_index("gx"), lax.axis_index("gy")
    nx = ngrp * ngx
    xt = grp * ngx + gx

    def dev(dx, dy):
        other = lax.rem(xt + dx + nx, nx)
        return (lax.div(other, ngx), lax.rem(other, ngx), lax.rem(gy + dy + ngy, ngy))

    barrier = pltpu.get_barrier_semaphore()
    everyone = nx * ngy

    def other(o):
        return dev(lax.div(o, ngy), lax.rem(o, ngy))

    def greet(o, c):
        pl.semaphore_signal(barrier, inc=1, device_id=other(o), device_id_type=MESH)
        return c

    lax.fori_loop(1, everyone, greet, 0)

    own = slice(HY, HY + cy)

    def stage(x):
        tt, qq, uu, vv = t_ref[x], q_ref[x], u_ref[x], v_ref[x]
        lift = w_ref[x] + DT * (THERMAL_LIFT * tt + HUMID_LIFT * qq)
        ue[x + H, own, :] = uu
        ve[x + H, own, :] = vv
        le[x + H, own, :] = lift
        te[x + H, own, :] = tt
        qe[x + H, own, :] = qq
        pack[0, x, 0:4, :] = uu[cy - 4 :]
        pack[0, x, 4:9, :] = vv[cy - 5 :]
        pack[0, x, 9:13, :] = lift[cy - 4 :]
        pack[0, x, 13:14, :] = tt[cy - 1 :]
        pack[0, x, 14:15, :] = qq[cy - 1 :]
        pack[1, x, 0:4, :] = uu[0:4]
        pack[1, x, 4:9, :] = vv[0:5]
        pack[1, x, 9:13, :] = lift[0:4]
        pack[1, x, 13:14, :] = tt[0:1]
        pack[1, x, 14:15, :] = qq[0:1]

    sweep(0, cx, stage)
    pl.semaphore_wait(barrier, everyone - 1)

    sems = [0]
    started = []

    def send(src, dst, target):
        i = sems[0]
        sems[0] += 1
        copy = pltpu.make_async_remote_copy(
            src_ref=src, dst_ref=dst, send_sem=send_sem.at[i], recv_sem=recv_sem.at[i],
            device_id=target, device_id_type=MESH,
        )
        copy.start()
        started.append(copy)
        return copy

    e = H + cx
    halo = []
    east, west = dev(1, 0), dev(-1, 0)
    halo.append(send(u_ref.at[pl.ds(cx - 5, 5)], ue.at[pl.ds(0, 5), own], east))
    halo.append(send(u_ref.at[pl.ds(0, 5)], ue.at[pl.ds(e, 5), own], west))
    halo.append(send(v_ref.at[pl.ds(cx - 4, 4)], ve.at[pl.ds(1, 4), own], east))
    halo.append(send(v_ref.at[pl.ds(0, 4)], ve.at[pl.ds(e, 4), own], west))
    halo.append(send(le.at[pl.ds(e - 4, 4), own], le.at[pl.ds(1, 4), own], east))
    halo.append(send(le.at[pl.ds(H, 4), own], le.at[pl.ds(e, 4), own], west))
    halo.append(send(pack.at[0], got.at[0, pl.ds(H, cx)], dev(0, 1)))
    halo.append(send(pack.at[1], got.at[1, pl.ds(H, cx)], dev(0, -1)))
    for a, dy in ((0, 1), (1, -1)):
        halo.append(send(pack.at[a, pl.ds(cx - 4, 4)], got.at[a, pl.ds(1, 4)], dev(1, dy)))
        halo.append(send(pack.at[a, pl.ds(0, 4)], got.at[a, pl.ds(e, 4)], dev(-1, dy)))
    for src, dst in ((t_ref, te), (q_ref, qe)):
        halo.append(send(src.at[pl.ds(cx - 1, 1)], dst.at[pl.ds(H - 1, 1), own], east))
        halo.append(send(src.at[pl.ds(0, 1)], dst.at[pl.ds(e, 1), own], west))

    lane = lax.broadcasted_iota(jnp.int32, (1, nz), 1)
    height = lane.astype(jnp.float32)
    rho = jnp.exp(-(height + 0.5) / nz)
    face = jnp.where(lane < nz - 1, jnp.exp(-(height + 1.0) / nz), 0.0)
    face_dn = jnp.where(lane > 0, jnp.exp(-height / nz), 0.0)
    not_top = jnp.where(lane < nz - 1, 1.0, 0.0)
    not_bot = jnp.where(lane > 0, 1.0, 0.0)
    rho_up = jnp.where(lane < nz - 1, jnp.exp(-(height + 1.5) / nz), 0.0)
    rho_dn = jnp.where(lane > 0, jnp.exp(-(height - 0.5) / nz), 0.0)

    def up(f):
        return pltpu.roll(f, nz - 1, 1)

    def down(f):
        return pltpu.roll(f, 1, 1)

    for copy in halo:
        copy.wait_recv()

    def unpack(x):
        s, n = got[0, x], got[1, x]
        ue[x, HY - 4 : HY, :] = s[0:4]
        ve[x, HY - 5 : HY, :] = s[4:9]
        le[x, HY - 4 : HY, :] = s[9:13]
        te[x, HY - 1 : HY, :] = s[13:14]
        qe[x, HY - 1 : HY, :] = s[14:15]
        ue[x, HY + cy : HY + cy + 4, :] = n[0:4]
        ve[x, HY + cy : HY + cy + 5, :] = n[4:9]
        le[x, HY + cy : HY + cy + 4, :] = n[9:13]
        te[x, HY + cy : HY + cy + 1, :] = n[13:14]
        qe[x, HY + cy : HY + cy + 1, :] = n[14:15]

    sweep(1, cx + 2 * H - 1, unpack)

    def make_r(x):
        vv, ll = ve[x], le[x]
        horiz = (ue[x + 1] - ue[x - 1]) + (pltpu.roll(vv, rows - 1, 0) - pltpu.roll(vv, 1, 0))
        div = rho * (0.5 * horiz) + 0.5 * (rho_up * up(ll) - rho_dn * down(ll))
        p0[x] = div * (-1.0 / DT)

    sweep(1, cx + 2 * H - 1, make_r)

    diag = ((4.0 + HELMHOLTZ) * rho + face + face_dn) / 6.0 - 1.0
    rho6, face6, face_dn6 = rho / 6.0, face / 6.0, face_dn / 6.0

    def scaled(f, x):
        c = f[x]
        side = f[x + 1] + f[x - 1] + pltpu.roll(c, rows - 1, 0) + pltpu.roll(c, 1, 0)
        return diag * c - rho6 * side - face6 * up(c) - face_dn6 * down(c)

    def step1(x):
        p1[x] = scaled(p0, x)

    def step2(x):
        p2[x] = 2.0 * scaled(p1, x) - p0[x]

    def step3(x):
        p3[x] = 2.0 * scaled(p2, x) - p1[x]

    full = cx + 2 * H
    sweep(2, full - 2, step1)
    sweep(3, full - 3, step2)
    sweep(4, full - 4, step3)

    def dots(x, acc):
        a0, a1, a2, a3 = p0[x, own, :], p1[x, own, :], p2[x, own, :], p3[x, own, :]
        side = p3[x + 1, own, :] + p3[x - 1, own, :]
        side = side + p3[x, HY - 1 : HY + cy - 1, :] + p3[x, HY + 1 : HY + cy + 1, :]
        a4 = 2.0 * (diag * a3 - rho6 * side - face6 * up(a3) - face_dn6 * down(a3)) - a2
        pairs = ((a0, a0), (a0, a1), (a1, a1), (a1, a2), (a2, a2), (a2, a3), (a3, a3), (a3, a4))
        return tuple(s + f * g for s, (f, g) in zip(acc, pairs))

    def dots_two(i, acc):
        return dots(H + 2 * i + 1, dots(H + 2 * i, acc))

    acc = lax.fori_loop(0, cx // 2, dots_two, (jnp.zeros((cy, nz), jnp.float32),) * 8)
    if cx % 2:
        acc = dots(e - 1, acc)
    corner = lax.broadcasted_iota(jnp.int32, (8, nz), 0) == lax.broadcasted_iota(
        jnp.int32, (8, nz), 1
    )
    sums = jnp.concatenate([jnp.sum(a, axis=0, keepdims=True) for a in acc], axis=0)
    sums = jnp.sum(sums, axis=1, keepdims=True)
    part[...] = jnp.sum(jnp.where(corner, sums, 0.0), axis=0, keepdims=True)

    def share(o):
        return pltpu.make_async_remote_copy(
            src_ref=part, dst_ref=got_x.at[o - 1],
            send_sem=sum_send.at[o - 1], recv_sem=sum_recv.at[o - 1],
            device_id=other(o), device_id_type=MESH,
        )

    def share_start(o, c):
        share(o).start()
        return c

    def share_wait(o, c):
        share(o).wait()
        return c

    lax.fori_loop(1, everyone, share_start, 0)
    dpb = size_ref.shape[1]
    nrow = ngx * slots
    nlev = KHI - KLO
    narrow = lax.broadcasted_iota(jnp.int32, (cx, dpb), 0)
    place_of = lax.broadcasted_iota(jnp.int32, (1, dpb), 1)
    for r in range(nrow):
        cell = cell_ref[r : r + 1, :]
        hot_s[r] = jnp.where(narrow == cell // (2 * nz), 1.0, 0.0).astype(jnp.bfloat16)
        lev_s[r : r + 1, :] = (cell // nz) % 2 * nlev + cell % nz - KLO
        live_s[r : r + 1, :] = jnp.where(place_of < cnt_ref[0, r], 1.0, 0.0)
    lax.fori_loop(1, everyone, share_wait, 0)
    total = part[...]
    for o in range(everyone - 1):
        total = total + got_x[o]
    total = jnp.where(corner, total, 0.0)
    total = jnp.broadcast_to(jnp.sum(total, axis=1, keepdims=True), (8, nz))
    dot = [total[i : i + 1, :] for i in range(8)]
    m = [dot[0], dot[1]]
    for k in range(2, 8):
        m.append(2.0 * dot[k] - m[k % 2])
    c0, c1, c2, c3 = cg_coefficients(m)

    def potential(x):
        phi_s[x] = c0 * p0[x] + c1 * p1[x] + c2 * p2[x] + c3 * p3[x]

    sweep(H - 1, e + 1, potential)

    sub = lax.broadcasted_iota(jnp.int32, (cy, nz), 0)
    lanes = lax.broadcasted_iota(jnp.int32, (cy, nz), 1)
    half = nz // 2
    south = slice(HY - 1, HY + cy - 1)
    north = slice(HY + 1, HY + cy + 1)

    def advance(x):
        g = x + H
        phi = phi_s[g, own, :]
        u = ue[g, own, :] - (DT * 0.5) * (phi_s[g + 1, own, :] - phi_s[g - 1, own, :])
        v = ve[g, own, :] - (DT * 0.5) * (phi_s[g, north, :] - phi_s[g, south, :])
        w = le[g, own, :] - (DT * 0.5) * (not_top * up(phi) - not_bot * down(phi))
        uo_ref[x] = u
        vo_ref[x] = v
        wo_ref[x] = w
        u_p, u_m = jnp.maximum(u, 0.0), jnp.minimum(u, 0.0)
        v_p, v_m = jnp.maximum(v, 0.0), jnp.minimum(v, 0.0)
        w_p, w_m = jnp.maximum(w, 0.0) * not_bot, jnp.minimum(w, 0.0) * not_top

        def move(f):
            h = f[g, own, :]
            return h - DT * (
                u_p * (h - f[g - 1, own, :])
                + u_m * (f[g + 1, own, :] - h)
                + v_p * (h - f[g, south, :])
                + v_m * (f[g, north, :] - h)
                + w_p * (h - down(h))
                + w_m * (up(h) - h)
            )

        tt, qq = move(te), move(qe)
        to_ref[x] = tt
        qo_ref[x] = qq
        sat = qq * jnp.exp(-CLAUSIUS_FACTOR * tt) - 1.0
        both = jnp.where(
            lanes < half, pltpu.roll(sat, nz - KLO, 1), pltpu.roll(tt, nz - KLO + half, 1)
        )
        odd = pltpu.roll(pltpu.roll(both, cy - 1, 0), nlev, 1)
        packed[x] = jnp.where(lanes % half < nlev, both, odd)

    sweep(0, cx, advance)
    for x in range(cx):
        for b in range(NBD):
            blk[b, x : x + 1, :] = packed[x, 2 * b : 2 * b + 1, :]

    for r in range(nrow):
        o, t = r // slots, r % slots
        row = None
        for b in range(t, NBD, slots):
            term = jnp.where(map_ref[0, b] == o, 1.0, 0.0) * blk[b]
            row = term if row is None else row + term
        out1[r] = row

    def exchange(src, dst):
        copies = []
        for o in range(1, ngx):
            other = lax.rem(gx + o, ngx)
            copies.append(
                send(
                    src.at[pl.ds(other * slots, slots)],
                    dst.at[pl.ds(gx * slots, slots)],
                    (grp, other, gy),
                )
            )
        for t in range(slots):
            dst[gx * slots + t] = src[gx * slots + t]
        for copy in copies:
            copy.wait_recv()

    exchange(out1, in1)

    wide = lax.broadcasted_iota(jnp.int32, (half, dpb), 0)
    flip = (((0,), (0,)), ((), ()))
    f32 = jnp.float32
    for r in range(nrow):
        table, hot = in1[r], hot_s[r]
        big = table.astype(jnp.bfloat16)
        rest = table - big.astype(f32)
        mid = rest.astype(jnp.bfloat16)
        res = lax.dot_general(big, hot, flip, preferred_element_type=f32)
        res = res + lax.dot_general(mid, hot, flip, preferred_element_type=f32)
        mask = wide == lev_s[r : r + 1, :]
        sat_s[r : r + 1, :] = jnp.sum(jnp.where(mask, res[:half], 0.0), axis=0, keepdims=True)
        tmp_s[r : r + 1, :] = jnp.sum(jnp.where(mask, res[half:], 0.0), axis=0, keepdims=True)

    rate = (2.0 * SUB_STEP * GROWTH) * jnp.exp(GROWTH_SLOPE * tmp_s[...])
    gain = rate * sat_s[...]
    loss = rate * CURVATURE
    old = size_ref[...]
    x2 = old
    for _ in range(NSUB):
        x2 = jnp.maximum(x2 + gain - loss * lax.rsqrt(x2), FLOOR_SQUARE)
    alive = live_s[...] > 0.5
    new = jnp.where(alive, x2, old)
    so_ref[...] = new
    sat_s[...] = jnp.where(
        alive,
        CONDENSE * mult_ref[...] * (new * jnp.sqrt(new) - old * jnp.sqrt(old)),
        0.0,
    )

    across = (((1,), (1,)), ((), ()))
    for r in range(nrow):
        mass = sat_s[r : r + 1, :]
        big = mass.astype(jnp.bfloat16).astype(f32)
        mask = wide == lev_s[r : r + 1, :]
        hi = jnp.where(mask, big, 0.0).astype(jnp.bfloat16)
        lo = jnp.where(mask, mass - big, 0.0).astype(jnp.bfloat16)
        both = jnp.concatenate([hi, lo], axis=0)
        res = lax.dot_general(hot_s[r], both, across, preferred_element_type=f32)
        out2[r] = res + pltpu.roll(res, half, 1)

    exchange(out2, in2)

    for b in range(NBD):
        acc = None
        for o in range(ngx):
            term = jnp.where(map_ref[0, b] == o, 1.0, 0.0) * in2[o * slots + b % slots]
            acc = term if acc is None else acc + term
        cond[b] = acc
    for copy in started:
        copy.wait_send()


def finish(t_ref, q_ref, u_ref, v_ref, w_ref, s_ref, cond, to, qo, uo, vo, wo, so, grid_c):
    cx, cy, nz = t_ref.shape
    nlev = KHI - KLO
    uo[...] = u_ref[...]
    vo[...] = v_ref[...]
    wo[...] = w_ref[...]
    so[...] = s_ref[...]
    for x in range(cx):
        for b in range(NBD):
            line = cond[b, x : x + 1, :]
            grid_c[x, 2 * b : 2 * b + 1, :] = line
            grid_c[x, 2 * b + 1 : 2 * b + 2, :] = line
    even = lax.broadcasted_iota(jnp.int32, (cy, nz), 0) % 2 == 0
    lanes = lax.broadcasted_iota(jnp.int32, (cy, nz), 1)
    inside = (lanes >= KLO) & (lanes < KHI)

    def column(x):
        f = grid_c[x]
        f = jnp.where(even, pltpu.roll(f, KLO, 1), pltpu.roll(f, KLO - nlev, 1))
        f = jnp.where(inside, f, 0.0)
        to[x] = t_ref[x] + PHASE_WARMING * f
        qo[x] = q_ref[x] - f

    sweep(0, cx, column, 4)


def on_device(ngrp, ngx, ngy, t, q, u, v, w, owner, count, size, mult, cell):
    cx, cy, nz = t.shape
    nrow, dpb = size.shape[2:]
    slots = nrow // ngx
    ext = pltpu.VMEM((cx + 2 * H, cy + 2 * HY, nz), jnp.float32)
    rowbuf = pltpu.VMEM((nrow, cx, nz), jnp.float32)
    vec = pltpu.VMEM((nrow, dpb), jnp.float32)
    nsem = 16 + 2 * (ngx - 1)
    nsum = ngrp * ngx * ngy - 1
    grid = jax.ShapeDtypeStruct((cx, cy, nz), jnp.float32)
    vm = pl.BlockSpec(memory_space=pltpu.VMEM)
    sm = pl.BlockSpec(memory_space=pltpu.SMEM)
    flat = jax.ShapeDtypeStruct((nrow, dpb), jnp.float32)
    blocks = jax.ShapeDtypeStruct((NBD, cx, nz), jnp.float32)
    mid = pl.pallas_call(
        functools.partial(kernel, ngrp, ngx, ngy, slots),
        out_shape=(grid,) * 5 + (flat, blocks),
        in_specs=[vm] * 5 + [sm] * 2 + [vm] * 3,
        out_specs=(vm,) * 7,
        scratch_shapes=[
            ext, ext, ext, ext, ext, ext, ext, ext, ext, ext,
            pltpu.VMEM((2, cx, 16, nz), jnp.float32),
            pltpu.VMEM((2, cx + 2 * H, 16, nz), jnp.float32),
            pltpu.VMEM((1, nz), jnp.float32),
            pltpu.VMEM((nsum, 1, nz), jnp.float32),
            pltpu.VMEM((NBD, cx, nz), jnp.float32),
            rowbuf, rowbuf, vec, vec, vec,
            pltpu.VMEM((nrow, dpb), jnp.int32),
            pltpu.VMEM((nrow, cx, dpb), jnp.bfloat16),
            rowbuf, rowbuf,
            pltpu.VMEM((cx, cy, nz), jnp.float32),
            pltpu.SemaphoreType.DMA((nsem,)),
            pltpu.SemaphoreType.DMA((nsem,)),
            pltpu.SemaphoreType.DMA((nsum,)),
            pltpu.SemaphoreType.DMA((nsum,)),
        ],
        compiler_params=pltpu.CompilerParams(collective_id=0, has_side_effects=True),
        name="cloud_step",
    )(
        t, q, u, v, w, owner.reshape(1, -1), count.reshape(1, -1),
        size[0, 0], mult[0, 0], cell[0, 0],
    )
    outs = pl.pallas_call(
        finish,
        out_shape=(grid,) * 5 + (flat,),
        in_specs=[vm] * 7,
        out_specs=(vm,) * 6,
        scratch_shapes=[pltpu.VMEM((cx, cy, nz), jnp.float32)],
        name="finish",
    )(*mid)
    return outs[:5] + (outs[5][None, None],)


def solution(mesh):
    grid = P(("grp", "gx"), "gy", None)
    drop = P(("grp", "gx"), "gy", None, None)
    return jax.shard_map(
        functools.partial(on_device, mesh.shape["grp"], mesh.shape["gx"], mesh.shape["gy"]),
        mesh=mesh,
        in_specs=(grid,) * 7 + (drop,) * 3,
        out_specs=(grid,) * 5 + (drop,),
        check_vma=False,
    )
```
